32 devices in a mesh: section: 4 (over z), seq: 8 (over y, x, core).
Axes of the slice: x: 2, y: 2, z: 4, core: 2. Of those that a mesh axis runs over, the one named last changes fastest.
Arguments:
- input_in_transit: bfloat16 [4, 1024, 4096], P('section', 'seq'), may hold values from -6 to 6
- mixer_norm_gain: float32 [4, 4096], P('section'), may hold values from 0.5 to 1.5
- convolution_weight: float32 [4, 4, 4096], P('section'), may hold values from -3 to 3
- convolution_bias: float32 [4, 4096], P('section'), may hold values from -2 to 2
- input_projection: bfloat16 [4, 4096, 288], P('section', 'seq'), may hold values from -0.09375 to 0.09375
- step_size_projection: bfloat16 [4, 256, 4096], P('section', None, 'seq'), may hold values from -0.375 to 0.375
- step_size_bias: float32 [4, 4096], P('section'), may hold values from -6.9 to -2.3
- log_decay_rates: float32 [4, 4096, 16], P('section'), may hold values from 0 to 2.77
- mixer_skip_weight: float32 [4, 4096], P('section'), may hold values from 0.5 to 1.5
- expert_norm_gain: float32 [4, 4096], P('section'), may hold values from 0.1 to 1.9
- router: bfloat16 [4, 4096, 16], P('section'), may hold values from -0.09375 to 0.09375
- gate_weight: bfloat16 [4, 4096, 12288], P('section', None, 'seq'), may hold values from -0.09375 to 0.09375
- up_weight: bfloat16 [4, 4096, 12288], P('section', None, 'seq'), may hold values from -0.09375 to 0.09375
- down_weight: bfloat16 [4, 12288, 4096], P('section', 'seq'), may hold values from -0.0546875 to 0.0546875
- expert_index_table: int32 [2, 4, 1024, 2], P(None, 'section', 'seq'), may hold values from 0 to 15, as said below
Outputs:
- layer_out: bfloat16 [4, 1024, 4096], P('section', 'seq')
The draws below stay inside these ranges and needn't reach their ends.
Inputs may be any that keep to these rules, and one draw needn't show every extreme that they name: `expert_index_table`: each token names two different experts of the 16; for each step and section, expert 0 is named by at most 8 tokens of any one block of 128 tokens.
All inputs are finite; a program needn't handle non-finite values.
Results may differ from the reference program's by a relative error of at most 0.0086.
Values may be sent and summed in bfloat16 or wider, within the bound.
A program may use at most 128 MiB of HBM per device.

```python
import jax
import jax.numpy as jnp
from jax import lax

MODEL_DIM = 4096
NSTATE = 16
RANK = 256
KCONV = 4
FF = 12288
EXPERTS = 16
STEPS = 2
L_DEV = 128
SEQUENCE_LENGTH = 1024
CAP = 8
N_SECTION = 4
N_SEQ = 8


def draw_expert_index_table(key, part):
    block_total = STEPS * N_SECTION * (SEQUENCE_LENGTH // L_DEV)
    keys = jax.random.split(jax.random.fold_in(key, 7321), 7)
    counts = jax.random.randint(keys[0], (block_total,), CAP // 4, CAP + 1)
    full = jax.random.randint(keys[1], (block_total,), 0, 4) == 0
    forced = jax.random.randint(keys[2], (), 0, block_total)
    full = full | (jnp.arange(block_total, dtype=jnp.int32) == forced)
    counts = jnp.where(full, CAP, counts)
    scores = jax.random.randint(keys[3], (block_total, L_DEV), 0, 1 << 20) * L_DEV + jnp.arange(L_DEV, dtype=jnp.int32)[None, :]
    order = jnp.argsort(scores, axis=1, stable=True)
    ranks = jnp.argsort(order, axis=1, stable=True)
    chosen = ranks < counts[:, None]
    first = jax.random.randint(keys[4], (block_total, L_DEV), 1, EXPERTS)
    offset = jax.random.randint(keys[5], (block_total, L_DEV), 1, EXPERTS - 1)
    second = 1 + (first - 1 + offset) % (EXPERTS - 1)
    side = jax.random.randint(keys[6], (block_total, L_DEV), 0, 2)
    first = jnp.where(chosen & (side == 0), 0, first)
    second = jnp.where(chosen & (side == 1), 0, second)
    pair = jnp.stack([first, second], -1).astype(jnp.int32)
    return pair.reshape(STEPS, N_SECTION, SEQUENCE_LENGTH, 2)


def block_levels(own_key, extent, pieces, smallest, largest):
    def one(axis_at, parts):
        draws = jax.random.uniform(jax.random.fold_in(jax.random.fold_in(own_key, 6), axis_at), (parts,), jnp.float32, smallest / len(pieces), largest / len(pieces))
        return jnp.repeat(jnp.exp(draws), extent[axis_at] // parts).reshape((-1,) + (1,) * (len(extent) - axis_at - 1))

    loudness = one(*pieces[0])
    for cut in pieces[1:]:
        loudness = loudness * one(*cut)
    return loudness


def centred(rng, shape, scale, limit, pieces=(), kind=jnp.bfloat16):
    values = scale * jax.random.normal(rng, shape, jnp.float32)
    if pieces:
        values = values * block_levels(rng, shape, pieces, -0.22, 0.18)
    return jnp.clip(values, -limit, limit).astype(kind)


def setup_inputs(seed: int = 0) -> dict:
    arg_keys = jax.random.split(jax.random.key(seed), 16)
    input_in_transit = centred(arg_keys[0], (N_SECTION, SEQUENCE_LENGTH, MODEL_DIM), 1.0, 6.0, ((0, 4), (1, 8)))
    mixer_norm_gain = jnp.clip(1.0 + 0.1 * jax.random.normal(arg_keys[1], (N_SECTION, MODEL_DIM), jnp.float32), 0.5, 1.5)
    convolution_weight = centred(arg_keys[2], (N_SECTION, KCONV, MODEL_DIM), 0.5, 3.0, ((0, 4),), jnp.float32)
    convolution_bias = centred(arg_keys[3], (N_SECTION, MODEL_DIM), 0.3, 2.0, ((0, 4),), jnp.float32)
    input_projection = centred(arg_keys[4], (N_SECTION, MODEL_DIM, RANK + 2 * NSTATE), MODEL_DIM ** -0.5, 0.09375, ((0, 4), (1, 8)))
    step_size_projection = centred(arg_keys[5], (N_SECTION, RANK, MODEL_DIM), RANK ** -0.5, 0.375, ((0, 4), (2, 8)))
    step_size_bias = jnp.clip(-6.9 + 4.6000001430511475 * jax.random.uniform(arg_keys[6], (N_SECTION, MODEL_DIM), jnp.float32) ** block_levels(arg_keys[6], (N_SECTION, MODEL_DIM), ((0, 4),), -0.2, 0.2), -6.9, -2.3)
    log_decay_rates = jnp.clip(2.77 * jax.random.uniform(arg_keys[7], (N_SECTION, MODEL_DIM, NSTATE), jnp.float32) ** block_levels(arg_keys[7], (N_SECTION, MODEL_DIM, NSTATE), ((0, 4),), -0.2, 0.2), 0.0, 2.77)
    mixer_skip_weight = jnp.clip(0.5 + 1.0 * jax.random.uniform(arg_keys[8], (N_SECTION, MODEL_DIM), jnp.float32) ** block_levels(arg_keys[8], (N_SECTION, MODEL_DIM), ((0, 4),), -0.2, 0.2), 0.5, 1.5)
    expert_norm_gain = jnp.clip(1.0 + 0.18 * jax.random.normal(arg_keys[9], (N_SECTION, MODEL_DIM), jnp.float32), 0.1, 1.9)
    router = centred(arg_keys[10], (N_SECTION, MODEL_DIM, EXPERTS), MODEL_DIM ** -0.5, 0.09375, ((0, 4),))
    gate_weight = centred(arg_keys[11], (N_SECTION, MODEL_DIM, FF), MODEL_DIM ** -0.5, 0.09375, ((0, 4), (2, 8)))
    up_weight = centred(arg_keys[12], (N_SECTION, MODEL_DIM, FF), MODEL_DIM ** -0.5, 0.09375, ((0, 4), (2, 8)))
    down_weight = centred(arg_keys[13], (N_SECTION, FF, MODEL_DIM), FF ** -0.5, 0.0546875, ((0, 4), (1, 8)))
    expert_index_table = draw_expert_index_table(jax.random.fold_in(arg_keys[15], 71), 0)
    return dict(input_in_transit=input_in_transit, mixer_norm_gain=mixer_norm_gain, convolution_weight=convolution_weight, convolution_bias=convolution_bias, input_projection=input_projection, step_size_projection=step_size_projection, step_size_bias=step_size_bias, log_decay_rates=log_decay_rates, mixer_skip_weight=mixer_skip_weight, expert_norm_gain=expert_norm_gain, router=router, gate_weight=gate_weight, up_weight=up_weight, down_weight=down_weight, expert_index_table=expert_index_table)


def rms_scale(values, gain):
    as_float = values.astype(jnp.float32)
    return as_float * lax.rsqrt(lax.optimization_barrier(jnp.mean(as_float * as_float, axis=-1, keepdims=True)) + 1e-06) * gain

def mixer(layer_input, mixer_norm_gain, convolution_weight, convolution_bias, input_projection, step_size_projection, step_size_bias, log_decay_rates, mixer_skip_weight):
    length = layer_input.shape[0]
    normed = rms_scale(layer_input, mixer_norm_gain).astype(jnp.bfloat16)
    padded = jnp.concatenate([jnp.zeros((KCONV - 1, MODEL_DIM), jnp.bfloat16), normed], 0)
    convolved = convolution_bias
    for tap in range(KCONV):
        convolved = convolved + convolution_weight[tap] * padded[tap:tap + length].astype(jnp.float32)
    inner = jax.nn.silu(convolved)
    inner_b = inner.astype(jnp.bfloat16)
    projected = jnp.dot(inner_b, input_projection, preferred_element_type=jnp.float32)
    low_rank = projected[:, :RANK].astype(jnp.bfloat16)
    b_in = projected[:, RANK:RANK + NSTATE]
    c_out = projected[:, RANK + NSTATE:]
    step_size = jax.nn.softplus(jnp.dot(low_rank, step_size_projection, preferred_element_type=jnp.float32) + step_size_bias)
    decay_rates = -jnp.exp(log_decay_rates)

    def advance(state, row_items):
        dt_row, in_row, b_row, c_row = row_items
        state = jnp.exp(dt_row[:, None] * decay_rates) * state + (dt_row * in_row)[:, None] * b_row[None, :]
        return (state, lax.optimization_barrier(jnp.sum(state * c_row[None, :], axis=1)))
    _, scanned = lax.scan(advance, jnp.zeros((MODEL_DIM, NSTATE), jnp.float32), (step_size, inner, b_in, c_out))
    return (layer_input.astype(jnp.float32) + (scanned + mixer_skip_weight * inner)).astype(jnp.bfloat16)

def experts_ref(mixed_rows, expert_norm_gain, router, gate_weight, up_weight, down_weight, chosen_ids):
    length = mixed_rows.shape[0]
    moe_in = rms_scale(mixed_rows, expert_norm_gain).astype(jnp.bfloat16)
    logits = jnp.dot(moe_in, router, preferred_element_type=jnp.float32)
    first = jnp.take_along_axis(logits, chosen_ids[:, 0:1], 1)[:, 0]
    second = jnp.take_along_axis(logits, chosen_ids[:, 1:2], 1)[:, 0]
    weight_one = jax.nn.sigmoid(first - second)
    weight_two = 1.0 - weight_one
    route_weight = jnp.where(chosen_ids[:, 0] == 0, weight_one, jnp.where(chosen_ids[:, 1] == 0, weight_two, jnp.zeros_like(weight_one)))
    routed = ((chosen_ids[:, 0] == 0) | (chosen_ids[:, 1] == 0)).astype(jnp.int32)
    blocked = routed.reshape(N_SEQ, L_DEV)
    slot = (jnp.cumsum(blocked, 1) - blocked).reshape(-1).astype(jnp.int32)
    block_of = (jnp.arange(length, dtype=jnp.int32) // L_DEV).astype(jnp.int32)
    total_slots = N_SEQ * CAP
    target = jnp.where(routed == 1, block_of * CAP + slot, total_slots).astype(jnp.int32)
    table = jnp.full((total_slots + 1,), length, jnp.int32).at[target].set(jnp.arange(length, dtype=jnp.int32))[:total_slots]
    padded_in = jnp.concatenate([moe_in, jnp.zeros((1, MODEL_DIM), jnp.bfloat16)], 0)
    sectioned = jnp.take(padded_in, table, axis=0)
    width = FF // N_SEQ

    def slice_term(total, index):
        start = (index * width).astype(jnp.int32)
        gate_cols = lax.dynamic_slice_in_dim(gate_weight, start, width, 1)
        up_cols = lax.dynamic_slice_in_dim(up_weight, start, width, 1)
        down_rows = lax.dynamic_slice_in_dim(down_weight, start, width, 0)
        gate_part = jnp.dot(sectioned, gate_cols, preferred_element_type=jnp.float32)
        up_part = jnp.dot(sectioned, up_cols, preferred_element_type=jnp.float32)
        hidden = (jax.nn.silu(gate_part) * up_part).astype(jnp.bfloat16)
        partial_value = jnp.dot(hidden, down_rows, preferred_element_type=jnp.float32).astype(jnp.bfloat16)
        partial_value = lax.optimization_barrier(partial_value)
        return (total + partial_value.astype(jnp.float32), None)
    summed, _ = lax.scan(slice_term, jnp.zeros((total_slots, MODEL_DIM), jnp.float32), jnp.arange(N_SEQ, dtype=jnp.int32))
    expert_out = summed.astype(jnp.bfloat16)
    padded_out = jnp.concatenate([expert_out, jnp.zeros((1, MODEL_DIM), jnp.bfloat16)], 0)
    picked = jnp.take(padded_out, target, axis=0).astype(jnp.float32)
    combined = route_weight[:, None] * picked
    return (mixed_rows.astype(jnp.float32) + combined).astype(jnp.bfloat16)

def reference(input_in_transit, mixer_norm_gain, convolution_weight, convolution_bias, input_projection, step_size_projection, step_size_bias, log_decay_rates, mixer_skip_weight, expert_norm_gain, router, gate_weight, up_weight, down_weight, expert_index_table):
    present_value = [input_in_transit[section_index] for section_index in range(N_SECTION)]
    produced = present_value
    for step in range(STEPS):
        produced = []
        for section_index in range(N_SECTION):
            mixed_rows = mixer(present_value[section_index], mixer_norm_gain[section_index], convolution_weight[section_index], convolution_bias[section_index], input_projection[section_index], step_size_projection[section_index], step_size_bias[section_index], log_decay_rates[section_index], mixer_skip_weight[section_index])
            produced.append(experts_ref(mixed_rows, expert_norm_gain[section_index], router[section_index], gate_weight[section_index], up_weight[section_index], down_weight[section_index], expert_index_table[step, section_index]))
        present_value = [produced[(section_index - 1) % N_SECTION] for section_index in range(N_SECTION)]
    return jnp.stack(produced, 0)
```

```python
import functools

import jax
import jax.numpy as jnp
from jax import lax
from jax.experimental import pallas as pl
from jax.experimental.pallas import tpu as pltpu
from jax.sharding import PartitionSpec as P

STEPS = 2
LANES = 128
ROWS = 8
MESH = pl.DeviceIdType.MESH
VMEM_LIMIT = 48 * 1024 * 1024


def greet(axis):
    n, me = lax.axis_size(axis), lax.axis_index(axis)
    barrier = pltpu.get_barrier_semaphore()
    for k in range(1, n):
        pl.semaphore_signal(
            barrier, inc=1, device_id={axis: lax.rem(me + k, n)}, device_id_type=MESH
        )
    pl.semaphore_wait(barrier, n - 1)


def exchange_kernel(axis, src_at, dst_at, x_ref, o_ref, send_sem, recv_sem, local_sem):
    n, me = lax.axis_size(axis), lax.axis_index(axis)
    greet(axis)
    copies = []
    for k in range(1, n):
        peer = lax.rem(me + k, n)
        copy = pltpu.make_async_remote_copy(
            src_ref=src_at(x_ref, peer),
            dst_ref=dst_at(o_ref, me),
            send_sem=send_sem.at[k],
            recv_sem=recv_sem.at[k],
            device_id={axis: peer},
            device_id_type=MESH,
        )
        copy.start()
        copies.append(copy)
    own = pltpu.make_async_copy(src_at(x_ref, me), dst_at(o_ref, me), local_sem)
    own.start()
    own.wait()
    for copy in copies:
        copy.wait()


def exchange(x, shape, src_at, dst_at, axis, cid):
    n = lax.axis_size(axis)
    return pl.pallas_call(
        functools.partial(exchange_kernel, axis, src_at, dst_at),
        out_shape=jax.ShapeDtypeStruct(shape, x.dtype),
        in_specs=[pl.BlockSpec(memory_space=pl.ANY)],
        out_specs=pl.BlockSpec(memory_space=pl.ANY),
        scratch_shapes=[
            pltpu.SemaphoreType.DMA((n,)),
            pltpu.SemaphoreType.DMA((n,)),
            pltpu.SemaphoreType.DMA,
        ],
        compiler_params=pltpu.CompilerParams(collective_id=cid, has_side_effects=True),
        name=f"exchange_{cid}",
    )(x)


def scatter_sum_kernel(axis, src_at, x_ref, o_ref, held, send_sem, recv_sem, local_sem):
    n, me = lax.axis_size(axis), lax.axis_index(axis)
    greet(axis)
    copies = []
    for k in range(1, n):
        peer = lax.rem(me + k, n)
        copy = pltpu.make_async_remote_copy(
            src_ref=src_at(x_ref, peer),
            dst_ref=held.at[k],
            send_sem=send_sem.at[k],
            recv_sem=recv_sem.at[k],
            device_id={axis: peer},
            device_id_type=MESH,
        )
        copy.start()
        copies.append(copy)
    own = pltpu.make_async_copy(src_at(x_ref, me), held.at[0], local_sem)
    own.start()
    own.wait()
    total = held[0].astype(jnp.float32)
    for k in range(1, n):
        copies[k - 1].wait()
        total = total + held[k].astype(jnp.float32)
    o_ref[...] = total


def scatter_sum(x, shape, src_at, axis, cid):
    n = lax.axis_size(axis)
    return pl.pallas_call(
        functools.partial(scatter_sum_kernel, axis, src_at),
        out_shape=jax.ShapeDtypeStruct(shape, jnp.float32),
        in_specs=[pl.BlockSpec(memory_space=pl.ANY)],
        out_specs=pl.BlockSpec(memory_space=pltpu.VMEM),
        scratch_shapes=[
            pltpu.VMEM((n,) + shape, x.dtype),
            pltpu.SemaphoreType.DMA((n,)),
            pltpu.SemaphoreType.DMA((n,)),
            pltpu.SemaphoreType.DMA,
        ],
        compiler_params=pltpu.CompilerParams(collective_id=cid, has_side_effects=True),
        name=f"scatter_sum_{cid}",
    )(x)


def row_block(size):
    return lambda ref, i: ref.at[pl.ds(pl.multiple_of(i * size, size), size), :]


def column_block(size):
    return lambda ref, i: ref.at[:, pl.ds(pl.multiple_of(i * size, size), size)]


def whole(ref, i):
    return ref


def slot_of(ref, i):
    return ref.at[i]


def scan_kernel(nstate, dt_ref, x_ref, bc_ref, a_ref, o_ref, h_ref):
    @pl.when(pl.program_id(0) == 0)
    def _():
        h_ref[...] = jnp.zeros_like(h_ref)

    rates = a_ref[...]
    width = rates.shape[1]

    def block(i, h):
        at = pl.ds(pl.multiple_of(i * ROWS, ROWS), ROWS)
        dt = dt_ref[at, :]
        u = dt * x_ref[at, :]
        bc = bc_ref[i]
        rows = []
        for k in range(ROWS):
            d = jnp.broadcast_to(dt[k : k + 1], (nstate, width))
            v = jnp.broadcast_to(u[k : k + 1], (nstate, width))
            h = jnp.exp(d * rates) * h + v * bc[:nstate, k : k + 1]
            rows.append(jnp.sum(h * bc[nstate:, k : k + 1], axis=0, keepdims=True))
        o_ref[at, :] = jnp.concatenate(rows, 0)
        return h

    h_ref[...] = lax.fori_loop(0, dt_ref.shape[0] // ROWS, block, h_ref[...])


def selective_scan(dt, x, bc, rates):
    length, width = dt.shape
    nstate = rates.shape[0]
    chunk = 128
    return pl.pallas_call(
        functools.partial(scan_kernel, nstate),
        out_shape=jax.ShapeDtypeStruct((length, width), jnp.float32),
        grid=(length // chunk,),
        in_specs=[
            pl.BlockSpec((chunk, width), lambda i: (i, 0)),
            pl.BlockSpec((chunk, width), lambda i: (i, 0)),
            pl.BlockSpec((chunk // ROWS, 2 * nstate, ROWS), lambda i: (i, 0, 0)),
            pl.BlockSpec((nstate, width), lambda i: (0, 0)),
        ],
        out_specs=pl.BlockSpec((chunk, width), lambda i: (i, 0)),
        scratch_shapes=[pltpu.VMEM((nstate, width), jnp.float32)],
        cost_estimate=pl.CostEstimate(
            flops=6 * length * width * nstate,
            bytes_accessed=12 * length * width,
            transcendentals=length * width * nstate,
        ),
        name="selective_scan",
    )(dt, x, bc, rates)


def passed_along(x, axis):
    length = lax.axis_size(axis)
    return lax.ppermute(x, axis, [(i, (i + 1) % length) for i in range(length)])


def dispatch_of(ids, blocks, capacity):
    length = ids.shape[0]
    size = length // blocks
    routed = (ids[:, 0] == 0) | (ids[:, 1] == 0)
    counted = routed.astype(jnp.float32).reshape(blocks, size)
    before = jnp.tril(jnp.ones((size, size), jnp.float32), -1)
    rank = jnp.dot(counted, before.T).reshape(length)
    slot = rank.astype(jnp.int32) + (jnp.arange(length, dtype=jnp.int32) // size) * capacity
    chosen = (jnp.arange(blocks * capacity, dtype=jnp.int32)[:, None] == slot[None, :]) & routed[
        None, :
    ]
    return chosen.astype(jnp.bfloat16), routed


def body(
    input_in_transit,
    mixer_norm_gain,
    convolution_weight,
    convolution_bias,
    input_projection,
    step_size_projection,
    step_size_bias,
    log_decay_rates,
    mixer_skip_weight,
    expert_norm_gain,
    router,
    gate_weight,
    up_weight,
    down_weight,
    expert_index_table,
):
    n, me = lax.axis_size("seq"), lax.axis_index("seq")
    experts = router.shape[2]
    rows = input_in_transit.shape[1]
    model = input_in_transit.shape[2]
    nstate = log_decay_rates.shape[2]
    rank = step_size_projection.shape[1]
    kernel = convolution_weight.shape[1]
    capacity = rows // 16
    length, width = rows * n, model // n
    slots = capacity * n
    f32, bf16 = jnp.float32, jnp.bfloat16

    def own(weight, axis):
        return lax.dynamic_slice_in_dim(weight, me * width, width, axis)

    gain = own(mixer_norm_gain[0], 0)
    taps = own(convolution_weight[0], 1)
    conv_bias = own(convolution_bias[0], 0)
    dt_bias = own(step_size_bias[0], 0)
    rates = -jnp.exp(own(log_decay_rates[0], 0)).T
    skip = own(mixer_skip_weight[0], 0)
    columns = rank + 2 * nstate
    extra = -columns % LANES
    projection = jnp.pad(input_projection[0], ((0, 0), (0, extra)))

    tokens = input_in_transit[0]
    as_float = tokens.astype(f32)
    square = jnp.sum(as_float * as_float, axis=-1)
    ids = expert_index_table[:, 0].astype(f32)
    small = jnp.concatenate(
        [ids.transpose(0, 2, 1).reshape(2 * STEPS, rows), square[None]], 0
    )
    small = jnp.pad(small, ((0, -small.shape[0] % ROWS), (0, 0)))
    small = exchange(small, (n,) + small.shape, whole, slot_of, "seq", 1)
    square = small[:, 2 * STEPS].reshape(length)
    all_ids = small[:, : 2 * STEPS].reshape(n, STEPS, 2, rows).transpose(1, 0, 3, 2)
    all_ids = all_ids.reshape(STEPS, length, 2)
    present = exchange(
        tokens, (length, width), column_block(width), row_block(rows), "seq", 2
    )

    for step in range(STEPS):
        if step:
            as_float = present.astype(f32)
            part = jnp.sum(as_float * as_float, axis=-1).reshape(n, rows)
            part = jnp.pad(part, ((0, -n % ROWS), (0, 0)))
            part = exchange(part, (n,) + part.shape, whole, slot_of, "seq", 3)
            square = jnp.sum(part, axis=0)[:n].reshape(length)
        scale = lax.rsqrt(square / model + 1e-06)
        normed = (present.astype(f32) * scale[:, None] * gain).astype(bf16)
        padded = jnp.concatenate([jnp.zeros((kernel - 1, width), bf16), normed], 0)
        convolved = conv_bias
        for tap in range(kernel):
            convolved = convolved + taps[tap] * padded[tap : tap + length].astype(f32)
        inner = jax.nn.silu(convolved)
        partial = jnp.dot(inner.astype(bf16), projection, preferred_element_type=f32).astype(bf16)
        projected = scatter_sum(partial, (rows, columns + extra), row_block(rows), "seq", 4)
        maps = projected[:, rank:columns]
        coarse = maps.astype(bf16)
        fine = (maps - coarse.astype(f32)).astype(bf16)
        sent = jnp.concatenate([projected[:, :rank].astype(bf16), coarse, fine], 1)
        sent = jnp.pad(sent, ((0, 0), (0, -sent.shape[1] % LANES)))
        everyone = exchange(sent, (length, sent.shape[1]), whole, row_block(rows), "seq", 5)
        maps = everyone[:, rank:columns].astype(f32) + everyone[
            :, columns : columns + 2 * nstate
        ].astype(f32)
        bc = maps.reshape(length // ROWS, ROWS, 2 * nstate).transpose(0, 2, 1)
        step_size = jax.nn.softplus(
            jnp.dot(everyone[:, :rank], step_size_projection[0], preferred_element_type=f32)
            + dt_bias
        )
        scanned = selective_scan(step_size, inner, bc, rates)
        mixed = (present.astype(f32) + (scanned + skip * inner)).astype(bf16)
        dispatch, routed = dispatch_of(all_ids[step], n, capacity)
        picked = jnp.dot(dispatch, mixed, preferred_element_type=f32).astype(bf16)
        last = step + 1 == STEPS
        if not last:
            moved = passed_along(mixed, "section")
            moved_ids = passed_along(all_ids[step], "section")
        full = exchange(picked, (slots, model), whole, column_block(width), "seq", 6)
        full_float = full.astype(f32)
        moe_in = (
            full_float
            * lax.rsqrt(jnp.mean(full_float * full_float, axis=-1, keepdims=True) + 1e-06)
            * expert_norm_gain[0]
        ).astype(bf16)
        logits = jnp.dot(moe_in, router[0], preferred_element_type=f32)
        slot_ids = jnp.dot(dispatch, all_ids[step].astype(bf16), preferred_element_type=f32)
        one_hot = (
            slot_ids[:, :, None] == jnp.arange(experts, dtype=jnp.int32).astype(f32)
        ).astype(f32)
        first = jnp.sum(logits * one_hot[:, 0], axis=1)
        second = jnp.sum(logits * one_hot[:, 1], axis=1)
        weight_one = jax.nn.sigmoid(first - second)
        route = jnp.where(
            slot_ids[:, 0] == 0,
            weight_one,
            jnp.where(slot_ids[:, 1] == 0, 1.0 - weight_one, jnp.zeros_like(weight_one)),
        )
        gate_part = jnp.dot(moe_in, gate_weight[0], preferred_element_type=f32)
        up_part = jnp.dot(moe_in, up_weight[0], preferred_element_type=f32)
        hidden = (jax.nn.silu(gate_part) * up_part).astype(bf16)
        terms = jnp.dot(hidden, down_weight[0], preferred_element_type=f32).astype(bf16)
        expert_out = scatter_sum(terms, (slots, width), column_block(width), "seq", 7).astype(bf16)
        new_rows = (picked.astype(f32) + route[:, None] * expert_out.astype(f32)).astype(bf16)
        if not last:
            new_rows = passed_along(new_rows, "section")
            dispatch, routed = dispatch_of(moved_ids, n, capacity)
            mixed = moved
        placed = lax.dot_general(
            dispatch, new_rows, (((0,), (0,)), ((), ())), preferred_element_type=f32
        ).astype(bf16)
        present = jnp.where(routed[:, None], placed, mixed)
    produced = exchange(present, (rows, model), row_block(rows), column_block(width), "seq", 8)
    return produced[None]


def solution(mesh):
    return jax.shard_map(
        body,
        mesh=mesh,
        in_specs=(
            P("section", "seq", None),
            P("section", None),
            P("section", None, None),
            P("section", None),
            P("section", "seq", None),
            P("section", None, "seq"),
            P("section", None),
            P("section", None, None),
            P("section", None),
            P("section", None),
            P("section", None, None),
            P("section", None, "seq"),
            P("section", None, "seq"),
            P("section", "seq", None),
            P(None, "section", "seq", None),
        ),
        out_specs=P("section", "seq", None),
        check_vma=False,
    )
```

```python
import functools

import jax
import jax.numpy as jnp
from jax import lax
from jax.experimental import pallas as pl
from jax.experimental.pallas import tpu as pltpu
from jax.sharding import PartitionSpec as P

STEPS = 2
LANES = 128
ROWS = 8
LOG2E = 1.4426950408889634
MESH = pl.DeviceIdType.MESH
SMALL_VMEM = 8 * 1024 * 1024


def greet(axis):
    n, me = lax.axis_size(axis), lax.axis_index(axis)
    barrier = pltpu.get_barrier_semaphore()
    for k in range(1, n):
        pl.semaphore_signal(
            barrier, inc=1, device_id={axis: lax.rem(me + k, n)}, device_id_type=MESH
        )
    pl.semaphore_wait(barrier, n - 1)


def exchange_kernel(axis, parts, *refs):
    n, me = lax.axis_size(axis), lax.axis_index(axis)
    count = len(parts)
    send_sem, recv_sem, local_sem = refs[2 * count :]
    greet(axis)
    copies = []
    for k in range(1, n):
        peer = lax.rem(me + k, n)
        for p, (src_at, dst_at) in enumerate(parts):
            copy = pltpu.make_async_remote_copy(
                src_ref=src_at(refs[p], peer),
                dst_ref=dst_at(refs[count + p], me),
                send_sem=send_sem.at[p, k],
                recv_sem=recv_sem.at[p, k],
                device_id={axis: peer},
                device_id_type=MESH,
            )
            copy.start()
            copies.append(copy)
    for p, (src_at, dst_at) in enumerate(parts):
        own = pltpu.make_async_copy(
            src_at(refs[p], me), dst_at(refs[count + p], me), local_sem.at[p]
        )
        own.start()
        copies.append(own)
    for copy in copies:
        copy.wait()


def exchange(xs, shapes, parts, axis, cid):
    n, count = lax.axis_size(axis), len(xs)
    return pl.pallas_call(
        functools.partial(exchange_kernel, axis, parts),
        out_shape=[jax.ShapeDtypeStruct(shape, x.dtype) for x, shape in zip(xs, shapes)],
        in_specs=[pl.BlockSpec(memory_space=pl.ANY)] * count,
        out_specs=[pl.BlockSpec(memory_space=pl.ANY)] * count,
        scratch_shapes=[
            pltpu.SemaphoreType.DMA((count, n)),
            pltpu.SemaphoreType.DMA((count, n)),
            pltpu.SemaphoreType.DMA((count,)),
        ],
        compiler_params=pltpu.CompilerParams(
            collective_id=cid, has_side_effects=True, vmem_limit_bytes=SMALL_VMEM
        ),
        name=f"exchange_{cid}",
    )(*xs)


def spread(axis, block, place, o_ref, send_sem, recv_sem, relay_send, relay_recv, local_sem):
    n, me = lax.axis_size(axis), lax.axis_index(axis)
    partner = me + 1 - 2 * lax.rem(me, 2)

    def send(source, at, target, sent, received):
        copy = pltpu.make_async_remote_copy(
            src_ref=source,
            dst_ref=place(o_ref, at),
            send_sem=sent,
            recv_sem=received,
            device_id={axis: target},
            device_id_type=MESH,
        )
        copy.start()
        return copy

    far = [
        send(block, me, lax.rem(me + 2 * k, n), send_sem.at[k], recv_sem.at[k])
        for k in range(1, n // 2)
    ]
    near = [send(block, me, partner, relay_send.at[0], relay_recv.at[0])]
    own = pltpu.make_async_copy(block, place(o_ref, me), local_sem)
    own.start()
    for k in range(1, n // 2):
        far[k - 1].wait_recv()
        source = lax.rem(me + n - 2 * k, n)
        near.append(
            send(place(o_ref, source), source, partner, relay_send.at[k], relay_recv.at[k])
        )
    for copy in far:
        copy.wait_send()
    for copy in near:
        copy.wait()
    own.wait()


def spread_scratch(n):
    return [pltpu.SemaphoreType.DMA((n // 2,))] * 4 + [pltpu.SemaphoreType.DMA]


def gather_kernel(axis, place, x_ref, o_ref, *sems):
    greet(axis)
    spread(axis, x_ref, place, o_ref, *sems)


def gather(x, shape, place, axis, cid):
    return pl.pallas_call(
        functools.partial(gather_kernel, axis, place),
        out_shape=jax.ShapeDtypeStruct(shape, x.dtype),
        in_specs=[pl.BlockSpec(memory_space=pl.ANY)],
        out_specs=pl.BlockSpec(memory_space=pl.ANY),
        scratch_shapes=spread_scratch(lax.axis_size(axis)),
        compiler_params=pltpu.CompilerParams(
            collective_id=cid, has_side_effects=True, vmem_limit_bytes=SMALL_VMEM
        ),
        name=f"gather_{cid}",
    )(x)


def reduce_here(axis, src_at, x_ref, held, send_sem, recv_sem, local_sem):
    n, me = lax.axis_size(axis), lax.axis_index(axis)
    copies = []
    for k in range(1, n):
        peer = lax.rem(me + k, n)
        copy = pltpu.make_async_remote_copy(
            src_ref=src_at(x_ref, peer),
            dst_ref=held.at[k],
            send_sem=send_sem.at[k],
            recv_sem=recv_sem.at[k],
            device_id={axis: peer},
            device_id_type=MESH,
        )
        copy.start()
        copies.append(copy)
    own = pltpu.make_async_copy(src_at(x_ref, me), held.at[0], local_sem)
    own.start()
    own.wait()
    total = held[0].astype(jnp.float32)
    for k in range(1, n):
        copies[k - 1].wait()
        total = total + held[k].astype(jnp.float32)
    return total


def reduce_scratch(n, shape, dtype):
    return [
        pltpu.VMEM((n,) + shape, dtype),
        pltpu.SemaphoreType.DMA((n,)),
        pltpu.SemaphoreType.DMA((n,)),
        pltpu.SemaphoreType.DMA,
    ]


def scatter_sum_kernel(axis, src_at, x_ref, o_ref, *scratch):
    greet(axis)
    o_ref[...] = reduce_here(axis, src_at, x_ref, *scratch)


def scatter_sum(x, shape, src_at, axis, cid):
    return pl.pallas_call(
        functools.partial(scatter_sum_kernel, axis, src_at),
        out_shape=jax.ShapeDtypeStruct(shape, jnp.float32),
        in_specs=[pl.BlockSpec(memory_space=pl.ANY)],
        out_specs=pl.BlockSpec(memory_space=pltpu.VMEM),
        scratch_shapes=reduce_scratch(lax.axis_size(axis), shape, x.dtype),
        compiler_params=pltpu.CompilerParams(
            collective_id=cid, has_side_effects=True, vmem_limit_bytes=SMALL_VMEM
        ),
        name=f"scatter_sum_{cid}",
    )(x)


def project_kernel(axis, src_at, place, rank, x_ref, o_ref, held, s1, s2, s3, stage, *sems):
    greet(axis)
    total = reduce_here(axis, src_at, x_ref, held, s1, s2, s3)
    end = total.shape[0]
    stage[:end, :] = total.astype(jnp.bfloat16)
    maps = total[rank:]
    stage[end:, :] = (maps - maps.astype(jnp.bfloat16).astype(jnp.float32)).astype(jnp.bfloat16)
    spread(axis, stage, place, o_ref, *sems)


def project(x, rank, block, axis, cid):
    n, (rows, length) = lax.axis_size(axis), x.shape
    tall = 2 * rows - rank
    return pl.pallas_call(
        functools.partial(project_kernel, axis, column_block(block), column_block(block), rank),
        out_shape=jax.ShapeDtypeStruct((tall, length), x.dtype),
        in_specs=[pl.BlockSpec(memory_space=pl.ANY)],
        out_specs=pl.BlockSpec(memory_space=pl.ANY),
        scratch_shapes=reduce_scratch(n, (rows, block), x.dtype)
        + [pltpu.VMEM((tall, block), x.dtype)]
        + spread_scratch(n),
        compiler_params=pltpu.CompilerParams(
            collective_id=cid, has_side_effects=True, vmem_limit_bytes=SMALL_VMEM
        ),
        name=f"project_{cid}",
    )(x)


def row_block(size):
    return lambda ref, i: ref.at[pl.ds(pl.multiple_of(i * size, size), size), :]


def column_block(size):
    return lambda ref, i: ref.at[:, pl.ds(pl.multiple_of(i * size, size), size)]


def whole(ref, i):
    return ref


def slot_of(ref, i):
    return ref.at[i]


def folded(parts):
    sub = lax.broadcasted_iota(jnp.int32, parts[0].shape, 0)
    reach = ROWS // 2
    while reach:
        low = (sub // reach) % 2 == 0
        half = len(parts) // 2
        merged = []
        for a, b in zip(parts[:half], parts[half:]):
            keep = jnp.where(low, a, b)
            give = jnp.where(low, b, a)
            if reach == ROWS // 2:
                moved = pltpu.roll(give, reach, 0)
            else:
                moved = jnp.where(
                    low, pltpu.roll(give, ROWS - reach, 0), pltpu.roll(give, reach, 0)
                )
            merged.append(keep + moved)
        parts = merged
        reach //= 2
    return parts[0]


def scan_kernel(nstate, dt_ref, x_ref, bc_ref, a_ref, o_ref, h_ref):
    @pl.when(pl.program_id(0) == 0)
    def _():
        h_ref[...] = jnp.zeros_like(h_ref)

    groups = nstate // ROWS
    chunk = dt_ref.shape[0]
    tile = (ROWS, dt_ref.shape[1])
    rates = [a_ref[g * ROWS : (g + 1) * ROWS, :] for g in range(groups)]

    def block(i, states):
        states = list(states)
        base = pl.multiple_of(i * ROWS, ROWS)
        bc = pltpu.roll(bc_ref[...], lax.rem(chunk - i * ROWS, chunk), 1)
        parts = []
        for k in range(ROWS):
            d = jnp.broadcast_to(dt_ref[pl.ds(base + k, 1), :], tile)
            v = d * jnp.broadcast_to(x_ref[pl.ds(base + k, 1), :], tile)
            total = None
            for g in range(groups):
                b = bc[g * ROWS : (g + 1) * ROWS, k : k + 1]
                c = bc[nstate + g * ROWS : nstate + (g + 1) * ROWS, k : k + 1]
                states[g] = jnp.exp2(d * rates[g]) * states[g] + v * b
                term = states[g] * c
                total = term if total is None else total + term
            parts.append(total)
        o_ref[pl.ds(base, ROWS), :] = folded(parts)
        return tuple(states)

    states = tuple(h_ref[g * ROWS : (g + 1) * ROWS, :] for g in range(groups))
    states = lax.fori_loop(0, chunk // ROWS, block, states)
    for g in range(groups):
        h_ref[g * ROWS : (g + 1) * ROWS, :] = states[g]


def selective_scan(dt, x, bc, rates):
    length, width = dt.shape
    nstate = rates.shape[0]
    chunk = LANES
    return pl.pallas_call(
        functools.partial(scan_kernel, nstate),
        out_shape=jax.ShapeDtypeStruct((length, width), jnp.float32),
        grid=(length // chunk,),
        in_specs=[
            pl.BlockSpec((chunk, width), lambda i: (i, 0)),
            pl.BlockSpec((chunk, width), lambda i: (i, 0)),
            pl.BlockSpec((2 * nstate, chunk), lambda i: (0, i)),
            pl.BlockSpec((nstate, width), lambda i: (0, 0)),
        ],
        out_specs=pl.BlockSpec((chunk, width), lambda i: (i, 0)),
        scratch_shapes=[pltpu.VMEM((nstate, width), jnp.float32)],
        compiler_params=pltpu.CompilerParams(vmem_limit_bytes=SMALL_VMEM),
        cost_estimate=pl.CostEstimate(
            flops=6 * length * width * nstate,
            bytes_accessed=12 * length * width,
            transcendentals=length * width * nstate,
        ),
        name="selective_scan",
    )(dt, x, bc, rates)


def passed_along(x, axis):
    length = lax.axis_size(axis)
    return lax.ppermute(x, axis, [(i, (i + 1) % length) for i in range(length)])


def dispatch_of(ids, blocks, capacity):
    length = ids.shape[0]
    size = length // blocks
    routed = (ids[:, 0] == 0) | (ids[:, 1] == 0)
    counted = routed.astype(jnp.float32).reshape(blocks, size)
    before = jnp.tril(jnp.ones((size, size), jnp.float32), -1)
    rank = jnp.dot(counted, before.T).reshape(length)
    slot = rank.astype(jnp.int32) + (jnp.arange(length, dtype=jnp.int32) // size) * capacity
    chosen = (jnp.arange(blocks * capacity, dtype=jnp.int32)[:, None] == slot[None, :]) & routed[
        None, :
    ]
    return chosen.astype(jnp.bfloat16), routed


def body(
    input_in_transit,
    mixer_norm_gain,
    convolution_weight,
    convolution_bias,
    input_projection,
    step_size_projection,
    step_size_bias,
    log_decay_rates,
    mixer_skip_weight,
    expert_norm_gain,
    router,
    gate_weight,
    up_weight,
    down_weight,
    expert_index_table,
):
    n, me = lax.axis_size("seq"), lax.axis_index("seq")
    experts = router.shape[2]
    rows = input_in_transit.shape[1]
    model = input_in_transit.shape[2]
    nstate = log_decay_rates.shape[2]
    rank = step_size_projection.shape[1]
    kernel = convolution_weight.shape[1]
    capacity = rows // 16
    length, width = rows * n, model // n
    slots = capacity * n
    f32, bf16 = jnp.float32, jnp.bfloat16

    def own(weight, axis):
        return lax.dynamic_slice_in_dim(weight, me * width, width, axis)

    gain = own(mixer_norm_gain[0], 0)
    taps = own(convolution_weight[0], 1)
    conv_bias = own(convolution_bias[0], 0)
    dt_bias = own(step_size_bias[0], 0)
    rates = -LOG2E * jnp.exp(own(log_decay_rates[0], 0)).T
    skip = own(mixer_skip_weight[0], 0)
    columns = rank + 2 * nstate

    tokens = input_in_transit[0]
    as_float = tokens.astype(f32)
    square = jnp.sum(as_float * as_float, axis=-1)
    ids = expert_index_table[:, 0].astype(f32)
    small = jnp.concatenate(
        [ids.transpose(0, 2, 1).reshape(2 * STEPS, rows), square[None]], 0
    )
    small = jnp.pad(small, ((0, -small.shape[0] % ROWS), (0, 0)))
    small, present = exchange(
        [small, tokens],
        [(n,) + small.shape, (length, width)],
        [(whole, slot_of), (column_block(width), row_block(rows))],
        "seq",
        1,
    )
    square = small[:, 2 * STEPS].reshape(length)
    all_ids = small[:, : 2 * STEPS].reshape(n, STEPS, 2, rows).transpose(1, 0, 3, 2)
    all_ids = all_ids.reshape(STEPS, length, 2)
    for step in range(STEPS):
        if step:
            as_float = present.astype(f32)
            part = jnp.sum(as_float * as_float, axis=-1).reshape(n, rows)
            part = jnp.pad(part, ((0, -n % ROWS), (0, 0)))
            (part,) = exchange([part], [(n,) + part.shape], [(whole, slot_of)], "seq", 3)
            square = jnp.sum(part, axis=0)[:n].reshape(length)
        scale = lax.rsqrt(square / model + 1e-06)
        normed = (present.astype(f32) * scale[:, None] * gain).astype(bf16)
        padded = jnp.concatenate([jnp.zeros((kernel - 1, width), bf16), normed], 0)
        convolved = conv_bias
        for tap in range(kernel):
            convolved = convolved + taps[tap] * padded[tap : tap + length].astype(f32)
        inner = jax.nn.silu(convolved)
        partial = lax.dot_general(
            input_projection[0],
            inner.astype(bf16),
            (((0,), (1,)), ((), ())),
            preferred_element_type=f32,
        ).astype(bf16)
        everyone = project(partial, rank, rows, "seq", 4)
        bc = everyone[rank:columns].astype(f32) + everyone[columns:].astype(f32)
        step_size = jax.nn.softplus(
            lax.dot_general(
                everyone[:rank],
                step_size_projection[0],
                (((0,), (0,)), ((), ())),
                preferred_element_type=f32,
            )
            + dt_bias
        )
        scanned = selective_scan(step_size, inner, bc, rates)
        mixed = (present.astype(f32) + (scanned + skip * inner)).astype(bf16)
        dispatch, routed = dispatch_of(all_ids[step], n, capacity)
        picked = jnp.dot(dispatch, mixed, preferred_element_type=f32).astype(bf16)
        last = step + 1 == STEPS
        if not last:
            moved = passed_along(mixed, "section")
            moved_ids = passed_along(all_ids[step], "section")
        full = gather(picked, (slots, model), column_block(width), "seq", 6)
        if last:
            mixed = lax.all_to_all(
                mixed.reshape(n, rows, width), "seq", split_axis=0, concat_axis=0
            )
            mixed = mixed.transpose(1, 0, 2).reshape(rows, model)
        full_float = full.astype(f32)
        moe_in = (
            full_float
            * lax.rsqrt(jnp.mean(full_float * full_float, axis=-1, keepdims=True) + 1e-06)
            * expert_norm_gain[0]
        ).astype(bf16)
        logits = jnp.dot(moe_in, router[0], preferred_element_type=f32)
        slot_ids = jnp.dot(dispatch, all_ids[step].astype(bf16), preferred_element_type=f32)
        one_hot = (
            slot_ids[:, :, None] == jnp.arange(experts, dtype=jnp.int32).astype(f32)
        ).astype(f32)
        first = jnp.sum(logits * one_hot[:, 0], axis=1)
        second = jnp.sum(logits * one_hot[:, 1], axis=1)
        weight_one = jax.nn.sigmoid(first - second)
        route = jnp.where(
            slot_ids[:, 0] == 0,
            weight_one,
            jnp.where(slot_ids[:, 1] == 0, 1.0 - weight_one, jnp.zeros_like(weight_one)),
        )
        gate_part = jnp.dot(moe_in, gate_weight[0], preferred_element_type=f32)
        up_part = jnp.dot(moe_in, up_weight[0], preferred_element_type=f32)
        hidden = (jax.nn.silu(gate_part) * up_part).astype(bf16)
        terms = jnp.dot(hidden, down_weight[0], preferred_element_type=f32).astype(bf16)
        if last:
            terms = terms.reshape(n, capacity, model)
            expert_out = scatter_sum(terms, (capacity, model), slot_of, "seq", 8)
            dispatch = lax.dynamic_slice(
                dispatch, (me * capacity, me * rows), (capacity, rows)
            )
            routed = lax.dynamic_slice_in_dim(routed, me * rows, rows, 0)
            route = lax.dynamic_slice_in_dim(route, me * capacity, capacity, 0)
            picked = lax.dynamic_slice_in_dim(full, me * capacity, capacity, 0)
        else:
            expert_out = scatter_sum(terms, (slots, width), column_block(width), "seq", 7)
        expert_out = expert_out.astype(bf16).astype(f32)
        new_rows = (picked.astype(f32) + route[:, None] * expert_out).astype(bf16)
        if not last:
            new_rows = passed_along(new_rows, "section")
            dispatch, routed = dispatch_of(moved_ids, n, capacity)
            mixed = moved
        placed = lax.dot_general(
            dispatch, new_rows, (((0,), (0,)), ((), ())), preferred_element_type=f32
        ).astype(bf16)
        present = jnp.where(routed[:, None], placed, mixed)
    return present[None]


def solution(mesh):
    return jax.shard_map(
        body,
        mesh=mesh,
        in_specs=(
            P("section", "seq", None),
            P("section", None),
            P("section", None, None),
            P("section", None),
            P("section", "seq", None),
            P("section", None, "seq"),
            P("section", None),
            P("section", None, None),
            P("section", None),
            P("section", None),
            P("section", None, None),
            P("section", None, "seq"),
            P("section", None, "seq"),
            P("section", "seq", None),
            P(None, "section", "seq", None),
        ),
        out_specs=P("section", "seq", None),
        check_vma=False,
    )
```
